512 devices in a mesh: img: 16 (over x, y_lo, core), vol: 32 (over z, y_hi).
Axes of the slice: x: 4, y: 8 (y_hi: 4, y_lo: 2; y = y_hi * 2 + y_lo), z: 8, core: 2. Of those that a mesh axis runs over, the one named last changes fastest.
Arguments:
- volume: float32 [512, 16, 4, 256], P('vol', 'img'), may hold values from -6 to 6
- images: bfloat16 [16384, 8, 256], P(('img', 'vol')), may hold values from -6 to 6
- ctf: float32 [16384, 8, 128], P(('img', 'vol')), may hold values from -1 to 1
- noise_weight: float32 [16384, 8, 128], P(('img', 'vol')), may hold values from 0.025 to 8, as said below
- shifts: float32 [16384, 2, 32], P(('img', 'vol')), may hold values from -4 to 4
- orient: int32 [16384, 64], P(('img', 'vol')), may hold values from 0 to 191, all different within a row
- counts: int32 [16384], P(('img', 'vol')), may hold values from 1 to 64
- tile_map: int32 [192, 8, 8], replicated, may hold values from 0 to 32767
- interp: float32 [192, 8, 8], replicated, may hold values from 0.05 to 0.3
Outputs:
- real_space: float32 [2, 512, 16, 512], P(None, None, 'img', 'vol')
- evidence: float32 [16384], P(('img', 'vol'))
The draws below stay inside these ranges and needn't reach their ends.
Inputs may be any that keep to these rules, and one draw needn't show every extreme that they name: `orient`: the 64 entries of one image are different orientations. `noise_weight`: positive.
All inputs are finite; a program needn't handle non-finite values.
Results may differ from the reference program's by a relative error of at most 0.0068.
Values may be sent and summed in bfloat16 or wider, within the bound.
No kernel may reach another device: no remote copies, remote signals or barrier semaphores. Data moves between devices by JAX's collectives and lax.ppermute only.
A program may use at most 64 MiB of HBM per device.

```python
import math
import jax
import jax.numpy as jnp
from jax import lax

NZ = 512
NY = 512
BOX = 256
TL = 128
NQ = 4
XW = 16
NT = 32768
PT = 8
NO = 192
KT = 8
NTR = 32
OMAX = 64
IMG_DEV = 32
IMAGES = 16384
N_IMG = 16
N_VOL = 32


def draw_noise_weight(key, part):
    pixel_key = jax.random.fold_in(key, 11)
    image_key = jax.random.fold_in(key, 12)
    per_pixel = jnp.exp(jax.random.uniform(pixel_key, (IMAGES, PT, TL), jnp.float32, jnp.log(0.05), jnp.log(0.2)))
    image_scale = jnp.exp(jax.random.uniform(image_key, (IMAGES, 1, 1), jnp.float32, jnp.log(0.5), jnp.log(2.0)))
    return per_pixel * image_scale


def plant(values, stream_key, low, top_value):
    longest = values.shape.index(max(values.shape))
    spots = []
    for shift in (0, 1):
        where = [jax.random.randint(jax.random.fold_in(stream_key, axis), (), 0, length) for axis, length in enumerate(values.shape)]
        where[longest] = (where[longest] + shift) % values.shape[longest]
        spots.append(tuple(where))
    return values.at[spots[0]].set(low).at[spots[1]].set(top_value)


def steps_of(key, dims, split, least, top_value):
    gain = 1.0
    for dim, shards_of in split:
        draws = jax.random.uniform(jax.random.fold_in(jax.random.fold_in(key, 6), dim), (shards_of,), jnp.float32, least / len(split), top_value / len(split))
        gain = gain * jnp.repeat(jnp.exp(draws), dims[dim] // shards_of).reshape((-1,) + (1,) * (len(dims) - 1 - dim))
    return gain


def picks_of(rng, rows, number_of, top, lift):
    ranking = jax.random.permutation(jax.random.fold_in(rng, 1), number_of)
    pull = ranking
    for power in range(3):
        pull = pull * pull // number_of
    pull = pull * lift // number_of
    chance = jax.random.randint(jax.random.fold_in(rng, 2), (rows, number_of), 0, 4096) + pull
    sure = jax.random.permutation(jax.random.fold_in(rng, 3), rows)[jnp.arange(number_of) % rows]
    chance = jnp.where(jnp.arange(rows)[:, None] == sure[None, :], 1 << 14, chance)
    merit = chance * number_of + jnp.arange(number_of)
    return lax.top_k(merit.astype(jnp.int32), top)[1].astype(jnp.int32)


def gaussian(stream_key, dims, scale, reach, pieces=(), held_as=jnp.bfloat16):
    level = steps_of(stream_key, dims, pieces, -0.22, 0.18) if pieces else 1.0
    values = jax.random.normal(stream_key, dims, jnp.float32) * scale * level
    return jnp.minimum(jnp.maximum(values, -reach), reach).astype(held_as)


def setup_inputs(seed: int = 0) -> dict:
    arg_keys = jax.random.split(jax.random.key(seed), 10)
    volume = gaussian(arg_keys[0], (NZ, XW, NQ, 2 * TL), 1.0, 6.0, ((0, 32), (1, 16)), jnp.float32)
    images = gaussian(arg_keys[1], (IMAGES, PT, 2 * TL), 1.0, 6.0, ((0, 512),))
    ctf = jnp.clip(jax.random.uniform(arg_keys[2], (IMAGES, PT, TL), jnp.float32, -1.0, 1.0) * steps_of(arg_keys[2], (IMAGES, PT, TL), ((0, 512),), -0.4, 0.0), -1.0, 1.0)
    noise_weight = draw_noise_weight(jax.random.fold_in(arg_keys[9], 71), 0)
    shifts = jnp.clip(jax.random.uniform(arg_keys[4], (IMAGES, 2, NTR), jnp.float32, -4.0, 4.0) * steps_of(arg_keys[4], (IMAGES, 2, NTR), ((0, 512),), -0.4, 0.0), -4.0, 4.0)
    orient = picks_of(arg_keys[5], IMAGES, NO, OMAX, 2730)
    counts = plant(jax.random.randint(arg_keys[6], (IMAGES,), 1, OMAX + 1), jax.random.fold_in(arg_keys[6], 1), 1, OMAX).astype(jnp.int32)
    tile_map = plant(jax.random.randint(arg_keys[7], (NO, PT, KT), 0, NT), jax.random.fold_in(arg_keys[7], 1), 0, NT - 1).astype(jnp.int32)
    interp = jnp.clip(jax.random.uniform(arg_keys[8], (NO, PT, KT), jnp.float32, 0.05, 0.3), 0.05, 0.3)
    return {"volume": volume, "images": images, "ctf": ctf, "noise_weight": noise_weight, "shifts": shifts, "orient": orient, "counts": counts, "tile_map": tile_map, "interp": interp}


precise = lax.Precision.HIGHEST


def shifted_weighted(images, ctf, noise_weight, shifts):
    num_images, rows_per, width = images.shape
    tile_len = width // 2
    row_freq = jnp.arange(rows_per, dtype=jnp.float32) / BOX
    col_freq = jnp.arange(tile_len, dtype=jnp.float32) / BOX
    angle = (-2.0 * math.pi) * (shifts[:, 0, :, None, None] * col_freq[None, None, None, :] + shifts[:, 1, :, None, None] * row_freq[None, None, :, None])
    cosine = jnp.cos(angle)
    sine = jnp.sin(angle)
    real_part = images[:, None, :, :tile_len].astype(jnp.float32)
    imag_part = images[:, None, :, tile_len:].astype(jnp.float32)
    factor = (noise_weight * ctf)[:, None]
    moved_re = (real_part * cosine - imag_part * sine) * factor
    moved_im = (real_part * sine + imag_part * cosine) * factor
    joined = jnp.concatenate([moved_re, moved_im], axis=-1).astype(jnp.bfloat16)
    return joined.reshape(num_images * shifts.shape[2], rows_per * width)


def score_block(weighted, slice_mat, power, ctf, noise_weight, orient, counts, trials):
    num_images = ctf.shape[0]
    orients = slice_mat.shape[0]
    slots = orient.shape[1]
    cross = lax.dot_general(weighted, slice_mat, (((1,), (1,)), ((), ())), preferred_element_type=jnp.float32)
    cross = cross.reshape(num_images, trials, orients)
    squared = (noise_weight * ctf * ctf).reshape(num_images, -1)
    penalty = jnp.dot(0.5 * squared, power.T, precision=precise)
    score = cross - penalty[:, None, :]
    onehot = (orient[:, :, None] == jnp.arange(orients, dtype=jnp.int32)[None, None, :]).astype(jnp.float32)
    picked = jnp.einsum('ito,ijo->ijt', score, onehot, precision=precise)
    usable = jnp.arange(slots, dtype=jnp.int32)[None, :] < counts[:, None]
    logits = jnp.where(usable[:, :, None], picked, -jnp.inf)
    highest = jnp.max(logits, axis=(1, 2))
    expo = jnp.exp(logits - highest[:, None, None])
    total = jnp.sum(expo, axis=(1, 2))
    evidence = highest + jnp.log(total)
    gamma = expo / total[:, None, None]
    spread = jnp.einsum('ijt,ijo->ito', gamma, onehot, precision=precise)
    spread_low = spread.astype(jnp.bfloat16).reshape(num_images * trials, orients)
    back_data = lax.dot_general(spread_low, weighted, (((0,), (0,)), ((), ())), preferred_element_type=jnp.float32)
    back_weight = jnp.dot(jnp.sum(spread, axis=1).T, squared, precision=precise)
    return back_data, back_weight, evidence


def reference(volume, images, ctf, noise_weight, shifts, orient, counts, tile_map, interp):
    flat_tiles = volume.reshape(NZ * XW * NQ, 2 * TL)
    summed = jnp.zeros((NO, PT, 2 * TL), jnp.float32)
    for term_index in range(KT):
        summed = summed + interp[:, :, term_index, None] * jnp.take(flat_tiles, tile_map[:, :, term_index], axis=0)
    slices = summed.astype(jnp.bfloat16)
    slice_mat = slices.reshape(NO, PT * 2 * TL)
    widened = slices.astype(jnp.float32)
    power = (widened[:, :, :TL] ** 2 + widened[:, :, TL:] ** 2).reshape(NO, PT * TL)
    groups = N_IMG * N_VOL

    def one_block(carry, block):
        weighted = shifted_weighted(block[0], block[1], block[2], block[3])
        back_data, back_weight, evidence = score_block(weighted, slice_mat, power, block[1], block[2], block[4], block[5], NTR)
        return (carry[0] + back_data, carry[1] + back_weight), evidence

    start = (jnp.zeros((NO, PT * 2 * TL), jnp.float32), jnp.zeros((NO, PT * TL), jnp.float32))
    blocks = (images.reshape(groups, IMG_DEV, PT, 2 * TL), ctf.reshape(groups, IMG_DEV, PT, TL), noise_weight.reshape(groups, IMG_DEV, PT, TL), shifts.reshape(groups, IMG_DEV, 2, NTR), orient.reshape(groups, IMG_DEV, OMAX), counts.reshape(groups, IMG_DEV))
    (back_data, back_weight), evidence = lax.scan(one_block, start, blocks)
    data_rows = back_data.reshape(NO * PT, 2 * TL)
    weight_rows = back_weight.reshape(NO * PT, TL)
    tile_data = jnp.zeros((NT, 2 * TL), jnp.float32)
    tile_weight = jnp.zeros((NT, TL), jnp.float32)
    for term_index in range(KT):
        target = tile_map[:, :, term_index].reshape(-1)
        scaled = interp[:, :, term_index].reshape(-1, 1)
        tile_data = tile_data.at[target].add(scaled * data_rows)
        tile_weight = tile_weight.at[target].add(scaled * weight_rows)
    tile_data = tile_data.reshape(NZ, XW, NQ, 2 * TL)
    denominator = tile_weight.reshape(NZ, XW, NY) + 1.0
    field_re = tile_data[:, :, :, :TL].reshape(NZ, XW, NY) / denominator
    field_im = tile_data[:, :, :, TL:].reshape(NZ, XW, NY) / denominator
    field = lax.complex(field_re, field_im)
    result = jnp.fft.ifft(jnp.fft.ifft(field, axis=2, norm="ortho"), axis=0, norm="ortho")
    depth_pos = ((jnp.arange(NZ, dtype=jnp.int32) + NZ // 2) % NZ - NZ // 2).astype(jnp.float32) / NZ
    line_pos = ((jnp.arange(NY, dtype=jnp.int32) + NY // 2) % NY - NY // 2).astype(jnp.float32) / NY
    correction = (jnp.sinc(depth_pos) ** 2)[:, None, None] * (jnp.sinc(line_pos) ** 2)[None, None, :]
    real_space = jnp.stack([jnp.real(result) / correction, jnp.imag(result) / correction]).astype(jnp.float32)
    return real_space, evidence.reshape(IMAGES)
```

```python
import functools
import math

import jax
import jax.numpy as jnp
from jax import lax
from jax.experimental import pallas as pl
from jax.experimental.pallas import tpu as pltpu
from jax.sharding import PartitionSpec as P

BOX = 256
f32 = jnp.float32
bf16 = jnp.bfloat16
precise = lax.Precision.HIGHEST
LOWEST = -3.0e38


def cos_sin_turns(turns):
    u = (turns - jnp.round(turns)) * (-math.pi)
    v = u * u
    s = 1.0 / 6227020800.0
    for coefficient in (-39916800.0, 362880.0, -5040.0, 120.0, -6.0, 1.0):
        s = s * v + 1.0 / coefficient
    s = s * u
    c = 1.0 / 479001600.0
    for coefficient in (-3628800.0, 40320.0, -720.0, 24.0, -2.0, 1.0):
        c = c * v + 1.0 / coefficient
    return 1.0 - 2.0 * s * s, 2.0 * s * c


def weighted_kernel(images_ref, ctf_ref, noise_ref, shift_ref, out_ref):
    num_images, rows_per, tile_len = ctf_ref.shape
    trials = shift_ref.shape[0] // num_images

    def one_image(index, carry):
        base = pl.multiple_of(index * trials, trials)
        rows = pl.ds(base, trials)
        column = lax.broadcasted_iota(jnp.int32, (trials, tile_len), 1).astype(f32) * (1.0 / BOX)
        shift_x = jnp.broadcast_to(shift_ref[rows, 0:1], (trials, tile_len))
        shift_y = jnp.broadcast_to(shift_ref[rows, 1:2], (trials, tile_len))
        cosine, sine = cos_sin_turns(shift_x * column)
        step_cos, step_sin = cos_sin_turns(shift_y * (1.0 / BOX))
        image = images_ref[index].astype(f32)
        factor = ctf_ref[index] * noise_ref[index]
        real = image[:, :tile_len] * factor
        imag = image[:, tile_len:] * factor
        for p in range(rows_per):
            re = jnp.broadcast_to(real[p : p + 1, :], (trials, tile_len))
            im = jnp.broadcast_to(imag[p : p + 1, :], (trials, tile_len))
            out_ref[p, rows, :tile_len] = (re * cosine - im * sine).astype(bf16)
            out_ref[p, rows, tile_len:] = (re * sine + im * cosine).astype(bf16)
            if p + 1 < rows_per:
                cosine, sine = (
                    cosine * step_cos - sine * step_sin,
                    sine * step_cos + cosine * step_sin,
                )
        return carry

    lax.fori_loop(0, num_images, one_image, 0)


def expectation_kernel(
    weighted_ref, slices_ref, squared_ref, mask_ref, back_ref, evidence_ref,
    score_ref, spread_ref, columns_ref, penalty_ref,
):
    rows_per, num_rows, width = weighted_ref.shape
    num_images, orients = mask_ref.shape
    tile_len = width // 2
    trials = num_rows // num_images
    penalty = jnp.zeros((num_images, orients), f32)
    for p in range(rows_per):
        part = slices_ref[p * orients : (p + 1) * orients, :].astype(f32)
        power = part[:, :tile_len] ** 2 + part[:, tile_len:] ** 2
        penalty += lax.dot_general(
            0.5 * squared_ref[p], power, (((1,), (1,)), ((), ())),
            precision=precise, preferred_element_type=f32,
        )
    penalty_ref[...] = penalty
    chunk = 256
    for start in range(0, num_rows, chunk):
        total = jnp.zeros((chunk, orients), f32)
        for p in range(rows_per):
            total += lax.dot_general(
                weighted_ref[p, start : start + chunk, :],
                slices_ref[p * orients : (p + 1) * orients, :],
                (((1,), (1,)), ((), ())), preferred_element_type=f32,
            )
        for index in range(start // trials, (start + chunk) // trials):
            low = index * trials - start
            row = total[low : low + trials, :] - penalty_ref[index : index + 1, :]
            row = jnp.where(mask_ref[index : index + 1, :] > 0.0, row, LOWEST)
            score_ref[index * trials : (index + 1) * trials, :] = row
            columns_ref[index : index + 1, :] = jnp.max(row, axis=0, keepdims=True)
    highest = jnp.max(columns_ref[...], axis=1, keepdims=True)
    for index in range(num_images):
        rows = slice(index * trials, (index + 1) * trials)
        expo = jnp.exp(score_ref[rows, :] - highest[index : index + 1, :])
        score_ref[rows, :] = expo
        columns_ref[index : index + 1, :] = jnp.sum(expo, axis=0, keepdims=True)
    sums = jnp.sum(columns_ref[...], axis=1, keepdims=True)
    evidence_ref[...] = jnp.broadcast_to(highest + jnp.log(sums), evidence_ref.shape)
    inverse = 1.0 / sums
    columns_ref[...] = columns_ref[...] * inverse
    for index in range(num_images):
        rows = slice(index * trials, (index + 1) * trials)
        spread_ref[rows, :] = (score_ref[rows, :] * inverse[index : index + 1, :]).astype(bf16)
    spread = spread_ref[...]
    for p in range(rows_per):
        rows = slice(p * orients, (p + 1) * orients)
        back_ref[rows, :width] = lax.dot_general(
            spread, weighted_ref[p], (((0,), (0,)), ((), ())), preferred_element_type=f32
        ).astype(back_ref.dtype)
        back_ref[rows, width:] = lax.dot_general(
            columns_ref[...], squared_ref[p], (((0,), (0,)), ((), ())),
            precision=precise, preferred_element_type=f32,
        ).astype(back_ref.dtype)


VMEM = pltpu.VMEM


def weigh(images, ctf, noise_weight, shifts):
    num_images, rows_per, width = images.shape
    trials = shifts.shape[2]
    columns = jnp.transpose(shifts, (0, 2, 1)).reshape(num_images * trials, 2)
    return pl.pallas_call(
        weighted_kernel,
        out_shape=jax.ShapeDtypeStruct((rows_per, num_images * trials, width), bf16),
        in_specs=[pl.BlockSpec(memory_space=VMEM)] * 4,
        out_specs=pl.BlockSpec(memory_space=VMEM),
        compiler_params=pltpu.CompilerParams(vmem_limit_bytes=24 << 20),
        name="weigh",
    )(images, ctf, noise_weight, columns)


def expect(weighted, slices, squared, mask):
    rows_per, num_rows, width = weighted.shape
    num_images, orients = mask.shape
    return pl.pallas_call(
        expectation_kernel,
        out_shape=(
            jax.ShapeDtypeStruct((rows_per * orients, width + width // 2), bf16),
            jax.ShapeDtypeStruct((num_images, 128), f32),
        ),
        in_specs=[pl.BlockSpec(memory_space=VMEM)] * 4,
        out_specs=(pl.BlockSpec(memory_space=VMEM),) * 2,
        scratch_shapes=[
            VMEM((num_rows, orients), f32),
            VMEM((num_rows, orients), bf16),
            VMEM((num_images, orients), f32),
            VMEM((num_images, orients), f32),
        ],
        compiler_params=pltpu.CompilerParams(vmem_limit_bytes=40 << 20),
        name="expect",
    )(weighted, slices, squared, mask)


def dft_tables(length):
    steps = jnp.arange(length, dtype=jnp.int32)
    product = steps[:, None] * steps[None, :] % length
    angle = product.astype(f32) * (2.0 * math.pi / length)
    norming = 1.0 / math.sqrt(length)
    return (jnp.cos(angle) * norming, jnp.sin(angle) * norming)


def centred_sinc(positions, length):
    centred = ((positions + length // 2) % length - length // 2).astype(f32) / length
    return jnp.sinc(centred) ** 2


def exchange(pieces, axis):
    return lax.all_to_all(pieces, axis, split_axis=0, concat_axis=0, tiled=True)


def scatter_sum(pieces, axis):
    return jnp.sum(exchange(pieces, axis).astype(f32), axis=0)


def gather_all(piece, axis, count):
    return exchange(jnp.broadcast_to(piece[None], (count,) + piece.shape), axis)


def on_device(volume, images, ctf, noise_weight, shifts, orient, counts, tile_map, interp):
    n_vol = lax.axis_size("vol")
    n_img = lax.axis_size("img")
    vol_index = lax.axis_index("vol")
    img_index = lax.axis_index("img")
    slab_depth, planes_dev, per_line, width = volume.shape
    tile_len = width // 2
    planes_all = planes_dev * n_img
    depth_len = slab_depth * n_vol
    line_len = per_line * tile_len
    orients, rows_per, terms = tile_map.shape
    num_rows = orients * rows_per
    num_images = images.shape[0]
    tiles = slab_depth * planes_dev * per_line
    block = num_rows // n_img
    part = block // n_vol

    tile_of = jnp.transpose(tile_map, (2, 1, 0)).reshape(terms, num_rows)
    factor_of = jnp.transpose(interp, (2, 1, 0)).reshape(terms, num_rows)
    tile_depth = tile_of // (planes_all * per_line)
    tile_plane = tile_of // per_line % planes_all
    tile_quarter = tile_of % per_line
    owned = (tile_depth // slab_depth == vol_index) & (tile_plane // planes_dev == img_index)
    local = (
        (tile_quarter * planes_dev + tile_plane - img_index * planes_dev) * slab_depth
        + tile_depth - vol_index * slab_depth
    )
    local = jnp.where(owned, local, -1)
    hit = local[:, None, :] == jnp.arange(tiles, dtype=jnp.int32)[None, :, None]
    mixing = jnp.sum(jnp.where(hit, factor_of[:, None, :], 0.0), axis=0)
    flat_tiles = jnp.transpose(volume, (2, 1, 0, 3)).reshape(tiles, width)

    partial = lax.dot_general(
        mixing, flat_tiles, (((0,), (0,)), ((), ())), precision=precise
    )
    mine = scatter_sum(partial.reshape(n_img, block, width), "img")
    mine = scatter_sum(mine.reshape(n_vol, part, width), "vol").astype(bf16)
    mine = gather_all(mine, "vol", n_vol).reshape(block, width)
    slices = gather_all(mine, "img", n_img).reshape(num_rows, width)

    weighted = weigh(images, ctf, noise_weight, shifts)
    squared = jnp.transpose(noise_weight * ctf * ctf, (1, 0, 2))
    slots = orient.shape[1]
    usable = jnp.arange(slots, dtype=jnp.int32)[None, :] < counts[:, None]
    listed = jnp.where(usable, orient, -1)
    mask = jnp.max(
        (listed[:, :, None] == jnp.arange(orients, dtype=jnp.int32)).astype(f32), axis=1
    )
    back, evidence = expect(weighted, slices, squared, mask)

    full = width + tile_len
    rows = scatter_sum(back.reshape(n_img, block, full), "img")
    rows = scatter_sum(rows.reshape(n_vol, part, full), "vol")
    rows = gather_all(rows, "vol", n_vol).reshape(block, full).astype(bf16)
    rows = gather_all(rows, "img", n_img).reshape(num_rows, full)
    acc = jnp.dot(mixing, rows.astype(f32), precision=precise)
    acc = acc.reshape(per_line, planes_dev * slab_depth, full)
    denominator = acc[:, :, width:] + 1.0
    field_re = acc[:, :, :tile_len] / denominator
    field_im = acc[:, :, tile_len:width] / denominator
    cos_line, sin_line = (t.reshape(per_line, tile_len, line_len) for t in dft_tables(line_len))
    dot_line = functools.partial(jnp.einsum, "qzk,qkn->zn", precision=precise)
    lines_re = dot_line(field_re, cos_line) - dot_line(field_im, sin_line)
    lines_im = dot_line(field_re, sin_line) + dot_line(field_im, cos_line)
    y_block = line_len // n_vol
    stacked = jnp.stack([lines_re, lines_im]).reshape(2, planes_dev, slab_depth, n_vol, y_block)
    stacked = jnp.transpose(stacked, (3, 2, 0, 1, 4)).reshape(
        n_vol, slab_depth, 2 * planes_dev * y_block
    )
    columns = exchange(stacked, "vol").reshape(depth_len, 2 * planes_dev * y_block)
    cos_depth, sin_depth = dft_tables(depth_len)
    by_cos = jnp.dot(cos_depth, columns, precision=precise)
    by_sin = jnp.dot(sin_depth, columns, precision=precise)
    half = planes_dev * y_block
    out_re = (by_cos[:, :half] - by_sin[:, half:]).reshape(depth_len, planes_dev, y_block)
    out_im = (by_sin[:, :half] + by_cos[:, half:]).reshape(depth_len, planes_dev, y_block)
    depth_corr = centred_sinc(jnp.arange(depth_len, dtype=jnp.int32), depth_len)
    line_corr = centred_sinc(vol_index * y_block + jnp.arange(y_block, dtype=jnp.int32), line_len)
    correction = depth_corr[:, None, None] * line_corr[None, None, :]
    real_space = jnp.stack([out_re / correction, out_im / correction])
    return (real_space, evidence[:, 0])


def solution(mesh):
    placed = (
        P("vol", "img", None, None),
        P(("img", "vol"), None, None),
        P(("img", "vol"), None, None),
        P(("img", "vol"), None, None),
        P(("img", "vol"), None, None),
        P(("img", "vol"), None),
        P(("img", "vol")),
        P(),
        P(),
    )
    return jax.shard_map(
        on_device,
        mesh=mesh,
        in_specs=placed,
        out_specs=(P(None, None, "img", "vol"), P(("img", "vol"))),
        check_vma=False,
    )
```

```python
import functools
import math

import jax
import jax.numpy as jnp
from jax import lax
from jax.experimental import pallas as pl
from jax.experimental.pallas import tpu as pltpu
from jax.sharding import PartitionSpec as P

BOX = 256
f32 = jnp.float32
bf16 = jnp.bfloat16
precise = lax.Precision.HIGHEST
LOWEST = -3.0e38


def cos_sin_turns(turns):
    u = (turns - jnp.round(turns)) * (-math.pi)
    v = u * u
    s = 1.0 / 6227020800.0
    for coefficient in (-39916800.0, 362880.0, -5040.0, 120.0, -6.0, 1.0):
        s = s * v + 1.0 / coefficient
    s = s * u
    c = 1.0 / 479001600.0
    for coefficient in (-3628800.0, 40320.0, -720.0, 24.0, -2.0, 1.0):
        c = c * v + 1.0 / coefficient
    return 1.0 - 2.0 * s * s, 2.0 * s * c


def weighted_kernel(images_ref, ctf_ref, noise_ref, shift_ref, out_ref):
    num_images, rows_per, tile_len = ctf_ref.shape
    trials = shift_ref.shape[0] // num_images

    def one_image(index, carry):
        base = pl.multiple_of(index * trials, trials)
        rows = pl.ds(base, trials)
        column = lax.broadcasted_iota(jnp.int32, (trials, tile_len), 1).astype(f32) * (1.0 / BOX)
        shift_x = jnp.broadcast_to(shift_ref[rows, 0:1], (trials, tile_len))
        shift_y = jnp.broadcast_to(shift_ref[rows, 1:2], (trials, tile_len))
        cosine, sine = cos_sin_turns(shift_x * column)
        step_cos, step_sin = cos_sin_turns(shift_y * (1.0 / BOX))
        image = images_ref[index].astype(f32)
        factor = ctf_ref[index] * noise_ref[index]
        real = image[:, :tile_len] * factor
        imag = image[:, tile_len:] * factor
        for p in range(rows_per):
            re = jnp.broadcast_to(real[p : p + 1, :], (trials, tile_len))
            im = jnp.broadcast_to(imag[p : p + 1, :], (trials, tile_len))
            out_ref[p, rows, :tile_len] = (re * cosine - im * sine).astype(bf16)
            out_ref[p, rows, tile_len:] = (re * sine + im * cosine).astype(bf16)
            if p + 1 < rows_per:
                cosine, sine = (
                    cosine * step_cos - sine * step_sin,
                    sine * step_cos + cosine * step_sin,
                )
        return carry

    lax.fori_loop(0, num_images, one_image, 0)


def expectation_kernel(
    core_ref, weighted_ref, near_ref, far_ref, squared_ref, mask_ref,
    send_ref, keep_ref, evidence_ref,
    score_ref, spread_ref, columns_ref, penalty_ref,
):
    rows_per, num_rows, width = weighted_ref.shape
    num_images, orients = mask_ref.shape
    half = rows_per // 2
    tile_len = width // 2
    trials = num_rows // num_images
    near_base = core_ref[0] * half
    far_base = (1 - core_ref[0]) * half
    halves = ((near_base, near_ref), (far_base, far_ref))
    penalty = jnp.zeros((num_images, orients), f32)
    for base, slices_ref in halves:
        for p in range(half):
            piece = slices_ref[p * orients : (p + 1) * orients, :].astype(f32)
            power = piece[:, :tile_len] ** 2 + piece[:, tile_len:] ** 2
            penalty += lax.dot_general(
                0.5 * squared_ref[base + p], power, (((1,), (1,)), ((), ())),
                precision=precise, preferred_element_type=f32,
            )
    penalty_ref[...] = penalty
    chunk = 256
    for start in range(0, num_rows, chunk):
        total = jnp.zeros((chunk, orients), f32)
        for base, slices_ref in halves:
            for p in range(half):
                total += lax.dot_general(
                    weighted_ref[base + p, start : start + chunk, :],
                    slices_ref[p * orients : (p + 1) * orients, :],
                    (((1,), (1,)), ((), ())), preferred_element_type=f32,
                )
        for index in range(start // trials, (start + chunk) // trials):
            low = index * trials - start
            row = total[low : low + trials, :] - penalty_ref[index : index + 1, :]
            row = jnp.where(mask_ref[index : index + 1, :] > 0.0, row, LOWEST)
            score_ref[index * trials : (index + 1) * trials, :] = row
            columns_ref[index : index + 1, :] = jnp.max(row, axis=0, keepdims=True)
    highest = jnp.max(columns_ref[...], axis=1, keepdims=True)
    for index in range(num_images):
        rows = slice(index * trials, (index + 1) * trials)
        expo = jnp.exp(score_ref[rows, :] - highest[index : index + 1, :])
        score_ref[rows, :] = expo
        columns_ref[index : index + 1, :] = jnp.sum(expo, axis=0, keepdims=True)
    sums = jnp.sum(columns_ref[...], axis=1, keepdims=True)
    evidence_ref[...] = jnp.broadcast_to(highest + jnp.log(sums), evidence_ref.shape)
    inverse = 1.0 / sums
    columns_ref[...] = columns_ref[...] * inverse
    for index in range(num_images):
        rows = slice(index * trials, (index + 1) * trials)
        spread_ref[rows, :] = (score_ref[rows, :] * inverse[index : index + 1, :]).astype(bf16)
    spread = spread_ref[...]
    for base, back_ref in ((far_base, send_ref), (near_base, keep_ref)):
        for p in range(half):
            rows = slice(p * orients, (p + 1) * orients)
            back_ref[rows, :width] = lax.dot_general(
                spread, weighted_ref[base + p], (((0,), (0,)), ((), ())),
                preferred_element_type=f32,
            ).astype(back_ref.dtype)
            back_ref[rows, width:] = lax.dot_general(
                columns_ref[...], squared_ref[base + p], (((0,), (0,)), ((), ())),
                precision=precise, preferred_element_type=f32,
            ).astype(back_ref.dtype)


def split(value):
    high = value.astype(bf16)
    return high, (value - high.astype(f32)).astype(bf16)


def dot_split(value, high_ref, low_ref):
    rows = value.shape[0]
    high, low = split(value)
    both = jnp.concatenate([high, low], axis=0)
    by_high = jnp.dot(both, high_ref[...], preferred_element_type=f32)
    by_low = jnp.dot(high, low_ref[...], preferred_element_type=f32)
    return by_high[:rows] + (by_high[rows:] + by_low)


def tables_kernel(cos_high_ref, cos_low_ref, sin_high_ref, sin_low_ref):
    length = cos_high_ref.shape[0]
    chunk = min(length, 64)

    def one_chunk(index, carry):
        base = pl.multiple_of(index * chunk, chunk)
        row = lax.broadcasted_iota(jnp.int32, (chunk, length), 0) + base
        column = lax.broadcasted_iota(jnp.int32, (chunk, length), 1)
        turns = (row * column % length).astype(f32) * (-1.0 / length)
        cosine, sine = cos_sin_turns(turns)
        rows = pl.ds(base, chunk)
        norming = 1.0 / math.sqrt(length)
        high, low = split(cosine * norming)
        cos_high_ref[rows, :] = high
        cos_low_ref[rows, :] = low
        high, low = split(sine * norming)
        sin_high_ref[rows, :] = high
        sin_low_ref[rows, :] = low
        return carry

    lax.fori_loop(0, length // chunk, one_chunk, 0)


def lines_kernel(
    mix_near_ref, mix_far_ref, near_ref, far_ref,
    cos_high_ref, cos_low_ref, sin_high_ref, sin_low_ref, out_ref,
):
    tiles = mix_near_ref.shape[0]
    full = near_ref.shape[1]
    tile_len = full // 3
    members, depth, packed = out_ref.shape
    per_line = tiles // depth
    total = jnp.zeros((2 * tiles, full), f32)
    for mix_ref, rows_ref in ((mix_near_ref, near_ref), (mix_far_ref, far_ref)):
        both = jnp.concatenate(split(mix_ref[...]), axis=0)
        total += jnp.dot(both, rows_ref[...], preferred_element_type=f32)
    acc = total[:tiles] + total[tiles:]
    real, imag = [], []
    for q in range(per_line):
        rows = slice(q * depth, (q + 1) * depth)
        denominator = acc[rows, 2 * tile_len :] + 1.0
        real.append(acc[rows, :tile_len] / denominator)
        imag.append(acc[rows, tile_len : 2 * tile_len] / denominator)
    field = jnp.concatenate(
        [jnp.concatenate(real, axis=1), jnp.concatenate(imag, axis=1)], axis=0
    )
    by_cos = dot_split(field, cos_high_ref, cos_low_ref)
    by_sin = dot_split(field, sin_high_ref, sin_low_ref)
    lines_re = by_cos[:depth] - by_sin[depth:]
    lines_im = by_sin[:depth] + by_cos[depth:]
    block = packed // 2
    for member in range(members):
        columns = slice(member * block, (member + 1) * block)
        out_ref[member, :, :block] = lines_re[:, columns]
        out_ref[member, :, block:] = lines_im[:, columns]


def depth_kernel(
    columns_ref, correction_ref, cos_high_ref, cos_low_ref, sin_high_ref, sin_low_ref, out_ref
):
    block = out_ref.shape[1]
    field = jnp.transpose(columns_ref[...])
    by_cos = dot_split(field, cos_high_ref, cos_low_ref)
    by_sin = dot_split(field, sin_high_ref, sin_low_ref)
    correction = correction_ref[...]
    out_ref[0] = (by_cos[:block] - by_sin[block:]) / correction
    out_ref[1] = (by_sin[:block] + by_cos[block:]) / correction


VMEM = pltpu.VMEM


def weigh(images, ctf, noise_weight, shifts):
    num_images, rows_per, width = images.shape
    trials = shifts.shape[2]
    columns = jnp.transpose(shifts, (0, 2, 1)).reshape(num_images * trials, 2)
    return pl.pallas_call(
        weighted_kernel,
        out_shape=jax.ShapeDtypeStruct((rows_per, num_images * trials, width), bf16),
        in_specs=[pl.BlockSpec(memory_space=VMEM)] * 4,
        out_specs=pl.BlockSpec(memory_space=VMEM),
        compiler_params=pltpu.CompilerParams(vmem_limit_bytes=24 << 20),
        name="weigh",
    )(images, ctf, noise_weight, columns)


def expect(core, weighted, near, far, squared, mask):
    rows_per, num_rows, width = weighted.shape
    num_images, orients = mask.shape
    half = jax.ShapeDtypeStruct((near.shape[0], width + width // 2), bf16)
    return pl.pallas_call(
        expectation_kernel,
        out_shape=(half, half, jax.ShapeDtypeStruct((num_images, 128), f32)),
        in_specs=[pl.BlockSpec(memory_space=pltpu.SMEM)] + [pl.BlockSpec(memory_space=VMEM)] * 5,
        out_specs=(pl.BlockSpec(memory_space=VMEM),) * 3,
        scratch_shapes=[
            VMEM((num_rows, orients), f32),
            VMEM((num_rows, orients), bf16),
            VMEM((num_images, orients), f32),
            VMEM((num_images, orients), f32),
        ],
        compiler_params=pltpu.CompilerParams(vmem_limit_bytes=24 << 20),
        name="expect",
    )(core, weighted, near, far, squared, mask)


def dft_tables(length):
    return pl.pallas_call(
        tables_kernel,
        out_shape=(jax.ShapeDtypeStruct((length, length), bf16),) * 4,
        out_specs=(pl.BlockSpec(memory_space=VMEM),) * 4,
        compiler_params=pltpu.CompilerParams(vmem_limit_bytes=8 << 20),
        name="tables",
    )()


def in_vmem(kernel, name, shape, *operands):
    return pl.pallas_call(
        kernel,
        out_shape=jax.ShapeDtypeStruct(shape, f32),
        in_specs=[pl.BlockSpec(memory_space=VMEM)] * len(operands),
        out_specs=pl.BlockSpec(memory_space=VMEM),
        compiler_params=pltpu.CompilerParams(vmem_limit_bytes=16 << 20),
        name=name,
    )(*operands)


def centred_sinc(positions, length):
    centred = ((positions + length // 2) % length - length // 2).astype(f32) / length
    return jnp.sinc(centred) ** 2


def exchange(pieces, axis):
    return lax.all_to_all(pieces, axis, split_axis=0, concat_axis=0, tiled=True)


def scatter_sum(pieces, axis):
    return jnp.sum(exchange(pieces, axis).astype(f32), axis=0)


def gather_all(piece, axis, count):
    return exchange(jnp.broadcast_to(piece[None], (count,) + piece.shape), axis)


def swap(value):
    return lax.ppermute(value, "core", [(0, 1), (1, 0)])


def on_device(volume, images, ctf, noise_weight, shifts, orient, counts, tile_map, interp):
    n_vol = lax.axis_size("vol")
    n_chip = lax.axis_size("chip")
    n_img = n_chip * 2
    vol_index = lax.axis_index("vol")
    core = lax.axis_index("core")
    img_index = lax.axis_index("chip") * 2 + core
    slab_depth, planes_dev, per_line, width = volume.shape
    tile_len = width // 2
    planes_all = planes_dev * n_img
    depth_len = slab_depth * n_vol
    line_len = per_line * tile_len
    orients, rows_per, terms = tile_map.shape
    half = orients * rows_per // 2
    slots = orient.shape[1]
    tiles = slab_depth * per_line
    block = half // n_chip
    part = block // n_vol
    full = width + tile_len

    tile_of = jnp.transpose(tile_map, (2, 1, 0)).reshape(terms, 2 * half)
    factor_of = jnp.transpose(interp, (2, 1, 0)).reshape(terms, 2 * half)
    tile_depth = tile_of // (planes_all * per_line)
    tile_plane = tile_of // per_line % planes_all
    tile_quarter = tile_of % per_line
    owned = (tile_depth // slab_depth == vol_index) & (tile_plane == img_index)
    local = jnp.where(owned, tile_quarter * slab_depth + tile_depth - vol_index * slab_depth, -1)

    def mixing_of(which):
        mine = lax.dynamic_slice_in_dim(local, which * half, half, axis=1)
        factor = lax.dynamic_slice_in_dim(factor_of, which * half, half, axis=1)
        hit = mine[:, None, :] == jnp.arange(tiles, dtype=jnp.int32)[None, :, None]
        return jnp.sum(jnp.where(hit, factor[:, None, :], 0.0), axis=0)

    mix_near = mixing_of(core)
    mix_far = mixing_of(1 - core)
    flat_tiles = jnp.transpose(volume, (2, 1, 0, 3)).reshape(tiles, width)
    mix_dot = functools.partial(
        lax.dot_general, dimension_numbers=(((0,), (0,)), ((), ())), precision=precise
    )
    mine = mix_dot(mix_near, flat_tiles) + swap(mix_dot(mix_far, flat_tiles))
    mine = scatter_sum(mine.reshape(n_chip, block, width), "chip")
    mine = scatter_sum(mine.reshape(n_vol, part, width), "vol").astype(bf16)
    mine = gather_all(mine, "vol", n_vol).reshape(block, width)
    near = gather_all(mine, "chip", n_chip).reshape(half, width)
    far = swap(near)

    weighted = weigh(images, ctf, noise_weight, shifts)
    squared = jnp.transpose(noise_weight * ctf * ctf, (1, 0, 2))
    usable = jnp.arange(slots, dtype=jnp.int32)[None, :] < counts[:, None]
    listed = jnp.where(usable, orient, -1)
    mask = jnp.max(
        (listed[:, :, None] == jnp.arange(orients, dtype=jnp.int32)).astype(f32), axis=1
    )
    tables_line = dft_tables(line_len)
    tables_depth = tables_line if depth_len == line_len else dft_tables(depth_len)
    send, keep, evidence = expect(
        core.astype(jnp.int32).reshape(1), weighted, near, far, squared, mask
    )

    rows = (keep.astype(f32) + swap(send).astype(f32)).astype(bf16)
    rows = scatter_sum(rows.reshape(n_chip, block, full), "chip")
    rows = scatter_sum(rows.reshape(n_vol, part, full), "vol").astype(bf16)
    rows = gather_all(rows, "vol", n_vol).reshape(block, full)
    rows_near = gather_all(rows, "chip", n_chip).reshape(half, full)
    rows_far = swap(rows_near)
    y_block = line_len // n_vol
    lines = in_vmem(
        lines_kernel, "lines", (n_vol, slab_depth, 2 * y_block),
        mix_near, mix_far, rows_near, rows_far, *tables_line,
    )
    columns = exchange(lines, "vol").reshape(depth_len, 2 * y_block)
    depth_corr = centred_sinc(jnp.arange(depth_len, dtype=jnp.int32), depth_len)
    line_corr = centred_sinc(vol_index * y_block + jnp.arange(y_block, dtype=jnp.int32), line_len)
    correction = line_corr[:, None] * depth_corr[None, :]
    real_space = in_vmem(
        depth_kernel, "depth", (2, y_block, depth_len), columns, correction, *tables_depth
    )
    return (jnp.transpose(real_space, (0, 2, 1))[:, :, None, :], evidence[:, 0])


def solution(mesh):
    devices = mesh.devices
    n_img, n_vol = devices.shape
    finer = jax.sharding.Mesh(devices.reshape(n_img // 2, 2, n_vol), ("chip", "core", "vol"))
    images = ("chip", "core", "vol")
    placed = (
        P("vol", ("chip", "core"), None, None),
        P(images, None, None),
        P(images, None, None),
        P(images, None, None),
        P(images, None, None),
        P(images, None),
        P(images),
        P(),
        P(),
    )
    return jax.shard_map(
        on_device,
        mesh=finer,
        in_specs=placed,
        out_specs=(P(None, None, ("chip", "core"), "vol"), P(images)),
        check_vma=False,
    )
```

```python
import functools
import math

import jax
import jax.numpy as jnp
from jax import lax
from jax.experimental import pallas as pl
from jax.experimental.pallas import tpu as pltpu
from jax.sharding import PartitionSpec as P

BOX = 256
f32 = jnp.float32
bf16 = jnp.bfloat16
precise = lax.Precision.HIGHEST
LOWEST = -3.0e38


def cos_sin_turns(turns):
    u = (turns - jnp.round(turns)) * (-math.pi)
    v = u * u
    s = 1.0 / 6227020800.0
    for coefficient in (-39916800.0, 362880.0, -5040.0, 120.0, -6.0, 1.0):
        s = s * v + 1.0 / coefficient
    s = s * u
    c = 1.0 / 479001600.0
    for coefficient in (-3628800.0, 40320.0, -720.0, 24.0, -2.0, 1.0):
        c = c * v + 1.0 / coefficient
    return 1.0 - 2.0 * s * s, 2.0 * s * c


def weighted_kernel(images_ref, ctf_ref, noise_ref, shift_ref, out_ref):
    num_images, rows_per, tile_len = ctf_ref.shape
    trials = shift_ref.shape[0] // num_images

    def one_image(index, carry):
        base = pl.multiple_of(index * trials, trials)
        rows = pl.ds(base, trials)
        column = lax.broadcasted_iota(jnp.int32, (trials, tile_len), 1).astype(f32) * (1.0 / BOX)
        shift_x = jnp.broadcast_to(shift_ref[rows, 0:1], (trials, tile_len))
        shift_y = jnp.broadcast_to(shift_ref[rows, 1:2], (trials, tile_len))
        cosine, sine = cos_sin_turns(shift_x * column)
        step_cos, step_sin = cos_sin_turns(shift_y * (1.0 / BOX))
        image = images_ref[index].astype(f32)
        factor = ctf_ref[index] * noise_ref[index]
        real = image[:, :tile_len] * factor
        imag = image[:, tile_len:] * factor
        for p in range(rows_per):
            re = jnp.broadcast_to(real[p : p + 1, :], (trials, tile_len))
            im = jnp.broadcast_to(imag[p : p + 1, :], (trials, tile_len))
            out_ref[p, rows, :tile_len] = (re * cosine - im * sine).astype(bf16)
            out_ref[p, rows, tile_len:] = (re * sine + im * cosine).astype(bf16)
            if p + 1 < rows_per:
                cosine, sine = (
                    cosine * step_cos - sine * step_sin,
                    sine * step_cos + cosine * step_sin,
                )
        return carry

    lax.fori_loop(0, num_images, one_image, 0)


def expectation_kernel(
    core_ref, weighted_ref, near_ref, far_ref, squared_ref, mask_ref,
    send_ref, keep_ref, evidence_ref,
    score_ref, spread_ref, columns_ref, penalty_ref,
):
    rows_per, num_rows, width = weighted_ref.shape
    num_images, orients = mask_ref.shape
    half = rows_per // 2
    tile_len = width // 2
    trials = num_rows // num_images
    near_base = core_ref[0] * half
    far_base = (1 - core_ref[0]) * half
    halves = ((near_base, near_ref), (far_base, far_ref))
    penalty = jnp.zeros((num_images, orients), f32)
    for base, slices_ref in halves:
        for p in range(half):
            piece = slices_ref[p * orients : (p + 1) * orients, :].astype(f32)
            power = piece[:, :tile_len] ** 2 + piece[:, tile_len:] ** 2
            penalty += lax.dot_general(
                0.5 * squared_ref[base + p], power, (((1,), (1,)), ((), ())),
                precision=precise, preferred_element_type=f32,
            )
    penalty_ref[...] = penalty
    chunk = 256
    for start in range(0, num_rows, chunk):
        total = jnp.zeros((chunk, orients), f32)
        for base, slices_ref in halves:
            for p in range(half):
                total += lax.dot_general(
                    weighted_ref[base + p, start : start + chunk, :],
                    slices_ref[p * orients : (p + 1) * orients, :],
                    (((1,), (1,)), ((), ())), preferred_element_type=f32,
                )
        for index in range(start // trials, (start + chunk) // trials):
            low = index * trials - start
            row = total[low : low + trials, :] - penalty_ref[index : index + 1, :]
            row = jnp.where(mask_ref[index : index + 1, :] > 0.0, row, LOWEST)
            score_ref[index * trials : (index + 1) * trials, :] = row
            columns_ref[index : index + 1, :] = jnp.max(row, axis=0, keepdims=True)
    highest = jnp.max(columns_ref[...], axis=1, keepdims=True)
    for index in range(num_images):
        rows = slice(index * trials, (index + 1) * trials)
        expo = jnp.exp(score_ref[rows, :] - highest[index : index + 1, :])
        score_ref[rows, :] = expo
        columns_ref[index : index + 1, :] = jnp.sum(expo, axis=0, keepdims=True)
    sums = jnp.sum(columns_ref[...], axis=1, keepdims=True)
    evidence_ref[...] = jnp.broadcast_to(highest + jnp.log(sums), evidence_ref.shape)
    inverse = 1.0 / sums
    columns_ref[...] = columns_ref[...] * inverse
    for index in range(num_images):
        rows = slice(index * trials, (index + 1) * trials)
        spread_ref[rows, :] = (score_ref[rows, :] * inverse[index : index + 1, :]).astype(bf16)
    spread = spread_ref[...]
    for base, back_ref in ((far_base, send_ref), (near_base, keep_ref)):
        for p in range(half):
            rows = slice(p * orients, (p + 1) * orients)
            back_ref[rows, :width] = lax.dot_general(
                spread, weighted_ref[base + p], (((0,), (0,)), ((), ())),
                preferred_element_type=f32,
            ).astype(back_ref.dtype)
            back_ref[rows, width:] = lax.dot_general(
                columns_ref[...], squared_ref[base + p], (((0,), (0,)), ((), ())),
                precision=precise, preferred_element_type=f32,
            ).astype(back_ref.dtype)


def split(value):
    high = value.astype(bf16)
    return high, (value - high.astype(f32)).astype(bf16)


def dot_split(value, high_ref, low_ref):
    rows = value.shape[0]
    high, low = split(value)
    both = jnp.concatenate([high, low], axis=0)
    by_high = jnp.dot(both, high_ref[...], preferred_element_type=f32)
    by_low = jnp.dot(high, low_ref[...], preferred_element_type=f32)
    return by_high[:rows] + (by_high[rows:] + by_low)


def tables_kernel(order_ref, cos_high_ref, cos_low_ref, sin_high_ref, sin_low_ref):
    length = cos_high_ref.shape[0]
    chunk = min(length, 64)

    def one_chunk(index, carry):
        base = pl.multiple_of(index * chunk, chunk)
        row = lax.broadcasted_iota(jnp.int32, (chunk, length), 0) + base
        column = lax.broadcasted_iota(jnp.int32, (chunk, length), 1)
        turns = (row * column % length).astype(f32) * (-1.0 / length)
        cosine, sine = cos_sin_turns(turns)
        rows = pl.ds(base, chunk)
        norming = 1.0 / math.sqrt(length)
        high, low = split(cosine * norming)
        cos_high_ref[rows, :] = high
        cos_low_ref[rows, :] = low
        high, low = split(sine * norming)
        sin_high_ref[rows, :] = high
        sin_low_ref[rows, :] = low
        return carry

    lax.fori_loop(0, length // chunk, one_chunk, 0)


def placing_kernel(index_ref, factor_ref, out_ref):
    terms = index_ref.shape[0]
    halves, tiles, half = out_ref.shape
    lanes, chunk = 128, 64
    for which in range(halves):
        for low in range(0, half, lanes):
            columns = slice(which * half + low, which * half + low + lanes)
            index = index_ref[:, columns]
            factor = factor_ref[:, columns]
            merged = jnp.zeros_like(factor)
            for k in range(terms):
                merged += jnp.where(index == index[k : k + 1, :], factor[k : k + 1, :], 0.0)
            index_of = [jnp.broadcast_to(index[k : k + 1, :], (8, lanes)) for k in range(terms)]
            value_of = [jnp.broadcast_to(merged[k : k + 1, :], (8, lanes)) for k in range(terms)]

            def one_chunk(step, carry):
                base = pl.multiple_of(step * chunk, chunk)
                row = lax.broadcasted_iota(jnp.int32, (8, lanes), 0) + base
                pieces = []
                for shift in range(0, chunk, 8):
                    value = jnp.zeros((8, lanes), f32)
                    for k in range(terms):
                        value = jnp.where(row + shift == index_of[k], value_of[k], value)
                    pieces.append(value)
                out_ref[which, pl.ds(base, chunk), low : low + lanes] = jnp.concatenate(
                    pieces, axis=0
                ).astype(bf16)
                return carry

            lax.fori_loop(0, tiles // chunk, one_chunk, 0)


def gather_kernel(place_scalar_ref, place_ref, rows_ref, acc_ref):
    tiles = acc_ref.shape[0]
    chunk = min(tiles, 256)
    core = place_scalar_ref[0]
    for low in range(0, tiles, chunk):
        acc_ref[low : low + chunk, :] = jnp.dot(
            place_ref[core, low : low + chunk, :], rows_ref[...], preferred_element_type=f32
        )


def finish_kernel(
    place_scalar_ref, place_ref, acc_ref, rows_ref, correction_ref,
    line_cos_high_ref, line_cos_low_ref, line_sin_high_ref, line_sin_low_ref,
    cos_high_ref, cos_low_ref, sin_high_ref, sin_low_ref, out_ref, field_ref,
):
    block, depth = correction_ref.shape
    tiles, full = acc_ref.shape
    tile_len = full // 3
    other = 1 - place_scalar_ref[0]
    first = pl.multiple_of(place_scalar_ref[1] * block, block)
    chosen = pl.ds(first, block)
    chunk = min(depth, 256)
    across = (((1,), (1,)), ((), ()))
    for z in range(0, depth, chunk):
        total_re = jnp.zeros((block, chunk), f32)
        total_im = jnp.zeros((block, chunk), f32)
        for q in range(tiles // depth):
            low = q * depth + z
            tile = acc_ref[low : low + chunk, :] + jnp.dot(
                place_ref[other, low : low + chunk, :], rows_ref[...], preferred_element_type=f32
            )
            columns = slice(q * tile_len, (q + 1) * tile_len)
            high_table = jnp.concatenate(
                [line_cos_high_ref[chosen, columns], line_sin_high_ref[chosen, columns]], axis=0
            )
            low_table = jnp.concatenate(
                [line_cos_low_ref[chosen, columns], line_sin_low_ref[chosen, columns]], axis=0
            )
            both_tables = jnp.concatenate([high_table, low_table], axis=0)
            inverse = 1.0 / (tile[:, 2 * tile_len :] + 1.0)
            parts = []
            for low_lane in (0, tile_len):
                high, low_part = split(tile[:, low_lane : low_lane + tile_len] * inverse)
                by_high = lax.dot_general(both_tables, high, across, preferred_element_type=f32)
                by_low = lax.dot_general(high_table, low_part, across, preferred_element_type=f32)
                parts.append(by_high[: 2 * block] + (by_high[2 * block :] + by_low))
            by_re, by_im = parts
            total_re += by_re[:block] - by_im[block:]
            total_im += by_re[block:] + by_im[:block]
        field_ref[:block, z : z + chunk] = total_re
        field_ref[block:, z : z + chunk] = total_im
    field = field_ref[...]
    by_cos = dot_split(field, cos_high_ref, cos_low_ref)
    by_sin = dot_split(field, sin_high_ref, sin_low_ref)
    correction = correction_ref[...]
    out_ref[0] = (by_cos[:block] - by_sin[block:]) / correction
    out_ref[1] = (by_sin[:block] + by_cos[block:]) / correction


VMEM = pltpu.VMEM


def weigh(images, ctf, noise_weight, shifts):
    num_images, rows_per, width = images.shape
    trials = shifts.shape[2]
    columns = jnp.transpose(shifts, (0, 2, 1)).reshape(num_images * trials, 2)
    return pl.pallas_call(
        weighted_kernel,
        out_shape=jax.ShapeDtypeStruct((rows_per, num_images * trials, width), bf16),
        in_specs=[pl.BlockSpec(memory_space=VMEM)] * 4,
        out_specs=pl.BlockSpec(memory_space=VMEM),
        compiler_params=pltpu.CompilerParams(vmem_limit_bytes=16 << 20),
        cost_estimate=pl.CostEstimate(
            flops=40 * rows_per * num_images * trials * width,
            bytes_accessed=2 * rows_per * num_images * trials * width, transcendentals=0,
        ),
        name="weigh",
    )(images, ctf, noise_weight, columns)


def expect(core, weighted, near, far, squared, mask):
    rows_per, num_rows, width = weighted.shape
    num_images, orients = mask.shape
    half = jax.ShapeDtypeStruct((near.shape[0], width + width // 2), bf16)
    return pl.pallas_call(
        expectation_kernel,
        out_shape=(half, half, jax.ShapeDtypeStruct((num_images, 128), f32)),
        in_specs=[pl.BlockSpec(memory_space=pltpu.SMEM)] + [pl.BlockSpec(memory_space=VMEM)] * 5,
        out_specs=(pl.BlockSpec(memory_space=VMEM),) * 3,
        scratch_shapes=[
            VMEM((num_rows, orients), f32),
            VMEM((num_rows, orients), bf16),
            VMEM((num_images, orients), f32),
            VMEM((num_images, orients), f32),
        ],
        compiler_params=pltpu.CompilerParams(vmem_limit_bytes=24 << 20),
        name="expect",
    )(core, weighted, near, far, squared, mask)


def dft_tables(order, length):
    return pl.pallas_call(
        tables_kernel,
        out_shape=(jax.ShapeDtypeStruct((length, length), bf16),) * 4,
        in_specs=[pl.BlockSpec(memory_space=pltpu.SMEM)],
        out_specs=(pl.BlockSpec(memory_space=VMEM),) * 4,
        compiler_params=pltpu.CompilerParams(vmem_limit_bytes=8 << 20),
        cost_estimate=pl.CostEstimate(flops=30 * length * length, bytes_accessed=8 * length * length, transcendentals=0),
        name="tables",
    )(order)


def in_vmem(kernel, name, out_shape, scalars, *operands, scratch=(), cost=None):
    return pl.pallas_call(
        kernel,
        out_shape=out_shape,
        in_specs=[pl.BlockSpec(memory_space=pltpu.SMEM)] * len(scalars)
        + [pl.BlockSpec(memory_space=VMEM)] * len(operands),
        out_specs=pl.BlockSpec(memory_space=VMEM),
        scratch_shapes=list(scratch),
        compiler_params=pltpu.CompilerParams(vmem_limit_bytes=24 << 20),
        cost_estimate=cost,
        name=name,
    )(*scalars, *operands)


def centred_sinc(positions, length):
    centred = ((positions + length // 2) % length - length // 2).astype(f32) / length
    return jnp.sinc(centred) ** 2


def exchange(pieces, axis):
    return lax.all_to_all(pieces, axis, split_axis=0, concat_axis=0, tiled=True)


def scatter_sum(pieces, axis):
    return jnp.sum(exchange(pieces, axis).astype(f32), axis=0)


def gather_all(piece, axis, count):
    return exchange(jnp.broadcast_to(piece[None], (count,) + piece.shape), axis)


def swap(value):
    return lax.ppermute(value, "core", [(0, 1), (1, 0)])


def on_device(volume, images, ctf, noise_weight, shifts, orient, counts, tile_map, interp):
    n_vol = lax.axis_size("vol")
    n_chip = lax.axis_size("chip")
    n_img = n_chip * 2
    vol_index = lax.axis_index("vol")
    core = lax.axis_index("core")
    img_index = lax.axis_index("chip") * 2 + core
    slab_depth, planes_dev, per_line, width = volume.shape
    tile_len = width // 2
    planes_all = planes_dev * n_img
    depth_len = slab_depth * n_vol
    line_len = per_line * tile_len
    orients, rows_per, terms = tile_map.shape
    half = orients * rows_per // 2
    slots = orient.shape[1]
    tiles = slab_depth * per_line
    block = half // n_chip
    part = block // n_vol
    full = width + tile_len

    tile_of = jnp.transpose(tile_map, (2, 1, 0)).reshape(terms, 2 * half)
    factor_of = jnp.transpose(interp, (2, 1, 0)).reshape(terms, 2 * half)
    tile_depth = tile_of // (planes_all * per_line)
    tile_plane = tile_of // per_line % planes_all
    tile_quarter = tile_of % per_line
    owned = (tile_depth // slab_depth == vol_index) & (tile_plane == img_index)
    local = jnp.where(owned, tile_quarter * slab_depth + tile_depth - vol_index * slab_depth, -1)

    def mixing_of(which):
        mine = lax.dynamic_slice_in_dim(local, which * half, half, axis=1)
        factor = lax.dynamic_slice_in_dim(factor_of, which * half, half, axis=1)
        hit = mine[:, None, :] == jnp.arange(tiles, dtype=jnp.int32)[None, :, None]
        return jnp.sum(jnp.where(hit, factor[:, None, :], 0.0), axis=0)

    mix_near = mixing_of(core)
    mix_far = mixing_of(1 - core)
    flat_tiles = jnp.transpose(volume, (2, 1, 0, 3)).reshape(tiles, width)
    mix_dot = functools.partial(
        lax.dot_general, dimension_numbers=(((0,), (0,)), ((), ())), precision=precise
    )
    mine = mix_dot(mix_near, flat_tiles) + swap(mix_dot(mix_far, flat_tiles))
    mine = scatter_sum(mine.reshape(n_chip, block, width), "chip")
    plane_index = jnp.where(tile_plane == img_index, tile_quarter * depth_len + tile_depth, -1)
    scalars = jnp.stack([core, vol_index]).astype(jnp.int32)
    pieces, plane_index, factor_in, order = lax.optimization_barrier(
        (mine.reshape(n_vol, part, width), plane_index, factor_of, scalars)
    )
    place = in_vmem(
        placing_kernel, "placing",
        jax.ShapeDtypeStruct((2, depth_len * per_line, half), bf16), (), plane_index, factor_in,
        cost=pl.CostEstimate(
            flops=40 * depth_len * per_line * half, bytes_accessed=4 * depth_len * per_line * half,
            transcendentals=0,
        ),
    )
    tables_line = dft_tables(order, line_len)
    tables_depth = tables_line if depth_len == line_len else dft_tables(order, depth_len)
    arrived = exchange(pieces, "vol")
    arrived, place, tables_line, tables_depth = lax.optimization_barrier(
        (arrived, place, tables_line, tables_depth)
    )
    mine = jnp.sum(arrived, axis=0).astype(bf16)
    pieces = jnp.broadcast_to(mine[None], (n_vol,) + mine.shape)
    pieces, images, ctf, noise_weight, shifts, orient, counts = lax.optimization_barrier(
        (pieces, images, ctf, noise_weight, shifts, orient, counts)
    )
    weighted = weigh(images, ctf, noise_weight, shifts)
    squared = jnp.transpose(noise_weight * ctf * ctf, (1, 0, 2))
    usable = jnp.arange(slots, dtype=jnp.int32)[None, :] < counts[:, None]
    listed = jnp.where(usable, orient, -1)
    mask = jnp.max(
        (listed[:, :, None] == jnp.arange(orients, dtype=jnp.int32)).astype(f32), axis=1
    )
    y_block = line_len // n_vol
    depth_corr = centred_sinc(jnp.arange(depth_len, dtype=jnp.int32), depth_len)
    line_corr = centred_sinc(vol_index * y_block + jnp.arange(y_block, dtype=jnp.int32), line_len)
    correction = line_corr[:, None] * depth_corr[None, :]
    arrived = exchange(pieces, "vol")
    arrived, weighted, squared, mask, correction = lax.optimization_barrier(
        (arrived, weighted, squared, mask, correction)
    )
    mine = arrived.reshape(block, width)
    near = gather_all(mine, "chip", n_chip).reshape(half, width)
    far = swap(near)

    send, keep, evidence = expect(scalars, weighted, near, far, squared, mask)

    rows = (keep.astype(f32) + swap(send).astype(f32)).astype(bf16)
    rows = scatter_sum(rows.reshape(n_chip, block, full), "chip")
    rows = scatter_sum(rows.reshape(n_vol, part, full), "vol").astype(bf16)
    rows = gather_all(rows, "vol", n_vol).reshape(block, full)
    rows_near = gather_all(rows, "chip", n_chip).reshape(half, full)
    rows_far = swap(rows_near)
    acc = in_vmem(
        gather_kernel, "gather", jax.ShapeDtypeStruct((depth_len * per_line, full), f32),
        (scalars,), place, rows_near,
        cost=pl.CostEstimate(
            flops=2 * depth_len * per_line * half * full,
            bytes_accessed=4 * depth_len * per_line * full, transcendentals=0,
        ),
    )
    real_space = in_vmem(
        finish_kernel, "finish", jax.ShapeDtypeStruct((2, y_block, depth_len), f32),
        (scalars,), place, acc, rows_far, correction, *tables_line, *tables_depth,
        scratch=(VMEM((2 * y_block, depth_len), f32),),
    )
    return (jnp.transpose(real_space, (0, 2, 1))[:, :, None, :], evidence[:, 0])


def solution(mesh):
    devices = mesh.devices
    n_img, n_vol = devices.shape
    finer = jax.sharding.Mesh(devices.reshape(n_img // 2, 2, n_vol), ("chip", "core", "vol"))
    images = ("chip", "core", "vol")
    placed = (
        P("vol", ("chip", "core"), None, None),
        P(images, None, None),
        P(images, None, None),
        P(images, None, None),
        P(images, None, None),
        P(images, None),
        P(images),
        P(),
        P(),
    )
    return jax.shard_map(
        on_device,
        mesh=finer,
        in_specs=placed,
        out_specs=(P(None, None, ("chip", "core"), "vol"), P(images)),
        check_vma=False,
    )
```
